32 devices in a mesh: angle: 8 (over z, x), row: 4 (over y, core).
Axes of the slice: x: 2, y: 2, z: 4, core: 2. Of those that a mesh axis runs over, the one named last changes fastest.
Arguments:
- raw_frames: bfloat16 [8, 8, 32, 2048], P('angle', None, 'row'), may hold values from 0.5 to 1.5
- step_index: int32 [8, 8], P('angle'), may hold values from 0 to 7, each once within a row
- partner: int32 [8], replicated, may hold values from 0 to 7, as said below
- flat_field: bfloat16 [2, 32, 2048], P(None, ('row', 'angle')), may hold values from -4 to 4
Outputs:
- filtered: bfloat16 [8, 32, 2048], P(None, ('row', 'angle'))
The draws below stay inside these ranges and needn't reach their ends.
Inputs may be any that keep to these rules, and one draw needn't show every extreme that they name: partner[partner[a]] = a, and every angle of the first half of the 8 angles is paired with one of the second half. `step_index`: each angle's row names every phase step once.
All inputs are finite; a program needn't handle non-finite values.
Results may differ from the reference program's by a relative error of at most 0.0078.
Values may be sent and summed in bfloat16 or wider, within the bound.
A program may use at most 128 MiB of HBM per device.

```python
import math
import jax
import jax.numpy as jnp
from jax import lax

DET = 2048
STEPS = 8
PAD = 4096
ANGLES = 8
ROWS = 32


def draw_partner(key, part):
    half = ANGLES // 2
    order = jax.random.permutation(jax.random.fold_in(key, 17), half).astype(jnp.int32)
    inverse = jnp.argsort(order).astype(jnp.int32)
    return jnp.concatenate([order + half, inverse]).astype(jnp.int32)


def level_of(rng, shape, shards, least, largest):
    gain = 1.0
    for axis_at, blocks in shards:
        draws = jax.random.uniform(jax.random.fold_in(jax.random.fold_in(rng, 6), axis_at), (blocks,), jnp.float32, least / len(shards), largest / len(shards))
        gain = gain * jnp.repeat(jnp.exp(draws), shape[axis_at] // blocks).reshape((-1,) + (1,) * (len(shape) - 1 - axis_at))
    return gain


def bell_draw(key, extent, deviation, most, cuts=(), kind=jnp.bfloat16):
    array = deviation * jax.random.normal(key, extent, jnp.float32)
    if cuts:
        array = array * level_of(key, extent, cuts, -0.22, 0.18)
    return jnp.clip(array, -most, most).astype(kind)


def setup_inputs(seed: int = 0) -> dict:
    splits = jax.random.split(jax.random.key(seed), 5)
    return {
        "raw_frames": jnp.clip(0.5 + 1.0 * jax.random.uniform(splits[0], (ANGLES, STEPS, ROWS, DET), jnp.float32) ** level_of(splits[0], (ANGLES, STEPS, ROWS, DET), ((0, 8), (2, 4)), -0.2, 0.2), 0.5, 1.5).astype(jnp.bfloat16),
        "step_index": jax.vmap(lambda own: jax.random.permutation(own, STEPS))(jax.random.split(splits[1], ANGLES)).reshape((ANGLES, STEPS)).astype(jnp.int32),
        "partner": draw_partner(jax.random.fold_in(splits[4], 71), 0),
        "flat_field": bell_draw(splits[3], (2, ROWS, DET), 1.0, 4.0, ((1, 32),)),
    }


two_pi = 2.0 * math.pi


def smooth_rows(field):
    padded = jnp.pad(field, ((0, 0), (1, 1), (0, 0)))
    return (0.25 * padded[:, :-2] + 0.5 * padded[:, 1:-1] + 0.25 * padded[:, 2:]).astype(jnp.bfloat16)


def reference(raw_frames, step_index, partner, flat_field):
    phase = step_index.astype(jnp.float32) * (two_pi / STEPS)
    weight_cos = jnp.cos(phase)
    weight_sin = jnp.sin(phase)
    corr_cos = jnp.zeros((ANGLES, ROWS, DET), jnp.float32)
    corr_sin = jnp.zeros((ANGLES, ROWS, DET), jnp.float32)
    corr_mean = jnp.zeros((ANGLES, ROWS, DET), jnp.float32)
    for step in range(STEPS):
        frame = raw_frames[:, step].astype(jnp.float32)
        corr_cos = corr_cos + frame * weight_cos[:, step][:, None, None]
        corr_sin = corr_sin + frame * weight_sin[:, step][:, None, None]
        corr_mean = corr_mean + frame
    smooth_cos = smooth_rows(corr_cos).astype(jnp.float32)
    smooth_sin = smooth_rows(corr_sin).astype(jnp.float32)
    smooth_mean = smooth_rows(corr_mean).astype(jnp.float32)
    flat = flat_field.astype(jnp.float32)
    dpc = (STEPS * (smooth_sin * flat[0][None] - smooth_cos * flat[1][None]) / smooth_mean).astype(jnp.bfloat16)
    mirror = jnp.take(dpc, partner.astype(jnp.int32), axis=0)[:, :, ::-1]
    combined = jnp.concatenate([-mirror, dpc], axis=2)
    column = lax.broadcasted_iota(jnp.int32, (PAD, DET), 0)
    freq = lax.broadcasted_iota(jnp.int32, (PAD, DET), 1)
    theta = ((column * freq) % PAD).astype(jnp.float32) * (two_pi / PAD)
    cos_table = jnp.cos(theta).astype(jnp.bfloat16)
    sin_table = jnp.sin(theta).astype(jnp.bfloat16)
    cos_own = cos_table[DET:]
    sin_own = sin_table[DET:]
    by_row = jnp.transpose(combined, (1, 0, 2))

    def filter_one(rows):
        spec_cos = jnp.dot(rows, cos_table, preferred_element_type=jnp.float32).astype(jnp.bfloat16)
        spec_sin = jnp.dot(rows, sin_table, preferred_element_type=jnp.float32).astype(jnp.bfloat16)
        first = jnp.dot(spec_cos, sin_own.T, preferred_element_type=jnp.float32)
        second = jnp.dot(spec_sin, cos_own.T, preferred_element_type=jnp.float32)
        return ((first - second) * (2.0 / PAD)).astype(jnp.bfloat16)

    filtered = lax.map(filter_one, by_row)
    return jnp.transpose(filtered, (1, 0, 2))
```

```python
import math

import jax
import jax.numpy as jnp
import ml_dtypes
import numpy as np
from jax import lax
from jax.sharding import PartitionSpec as P

two_pi = 2.0 * math.pi


def padded_2(block, sides, width):
    for axis, dim in sides:
        count = lax.axis_size(axis)
        forward = [(i, i + 1) for i in range(count - 1)]
        backward = [(target, source) for source, target in forward]
        low = lax.ppermute(
            lax.slice_in_dim(block, block.shape[dim] - width, None, axis=dim), axis, forward
        )
        high = lax.ppermute(lax.slice_in_dim(block, 0, width, axis=dim), axis, backward)
        block = jnp.concatenate([low, block, high], axis=dim)
    return block


def make_dpc(smooth_cos, smooth_sin, smooth_mean, flat, steps):
    flat_cos = flat[0].astype(jnp.float32)[None]
    flat_sin = flat[1].astype(jnp.float32)[None]
    value = steps * (
        smooth_sin.astype(jnp.float32) * flat_cos - smooth_cos.astype(jnp.float32) * flat_sin
    )
    return (value / smooth_mean.astype(jnp.float32)).astype(jnp.bfloat16)


def circulant_blocks(padlen, width):
    count = padlen // width
    n = np.arange(padlen, dtype=np.float64)
    odd = np.arange(padlen) % 2 == 1
    taps = np.where(odd, (2.0 / padlen) / np.tan(np.pi * np.where(odd, n, 1.0) / padlen), 0.0)
    m = np.arange(count)[:, None, None]
    p = np.arange(width)[None, :, None]
    q = np.arange(width)[None, None, :]
    return taps[(width * m + q - p) % padlen].astype(ml_dtypes.bfloat16)


def filter_rows(rows, det):
    width = 256
    count, padlen = rows.shape
    blocks = circulant_blocks(padlen, width)
    turns, own = padlen // width, det // width
    table = jnp.asarray(blocks.reshape(padlen, width))
    cut = rows.reshape(count, turns, width).transpose(1, 0, 2)
    cut = jnp.concatenate([cut, cut[: own - 1]], axis=0)
    starts = [(own - m) % turns for m in range(turns)]
    left = jnp.concatenate([cut[s : s + own] for s in starts], axis=2)
    total = jnp.dot(left.reshape(own * count, padlen), table, preferred_element_type=jnp.float32)
    return total.reshape(own, count, width).transpose(1, 0, 2).reshape(count, det).astype(jnp.bfloat16)


def local(raw_frames, step_index, partner, flat_field):
    ang_dev, steps, rows_blk, det = raw_frames.shape
    phase = step_index.astype(jnp.float32) * (two_pi / steps)
    weight_cos = jnp.cos(phase)
    weight_sin = jnp.sin(phase)
    corr_cos = jnp.zeros((ang_dev, rows_blk, det), jnp.float32)
    corr_sin = jnp.zeros((ang_dev, rows_blk, det), jnp.float32)
    corr_mean = jnp.zeros((ang_dev, rows_blk, det), jnp.float32)
    for step in range(steps):
        frame = raw_frames[:, step].astype(jnp.float32)
        corr_cos = corr_cos + frame * weight_cos[:, step][:, None, None]
        corr_sin = corr_sin + frame * weight_sin[:, step][:, None, None]
        corr_mean = corr_mean + frame
    stacked = jnp.stack([corr_cos, corr_sin, corr_mean])
    edges = jnp.concatenate([stacked[:, :, :1], stacked[:, :, -1:]], axis=2)
    rims = padded_2(edges, (("row", 2),), 1)
    padded = jnp.concatenate([rims[:, :, :1], stacked, rims[:, :, 3:]], axis=2)
    smoothed = (
        0.25 * padded[:, :, :-2] + 0.5 * padded[:, :, 1:-1] + 0.25 * padded[:, :, 2:]
    ).astype(jnp.bfloat16)
    flat_block = lax.all_gather(flat_field, "angle", axis=1, tiled=True)
    dpc = make_dpc(smoothed[0], smoothed[1], smoothed[2], flat_block, steps)
    dpc_all = lax.all_to_all(dpc, "angle", split_axis=1, concat_axis=0, tiled=True)
    angles_all, rows_here, _ = dpc_all.shape
    mirror = jnp.take(dpc_all, partner, axis=0)[:, :, ::-1]
    combined = jnp.concatenate([-mirror, dpc_all], axis=2)
    flat_rows = combined.reshape(angles_all * rows_here, 2 * det)
    result = filter_rows(flat_rows, det)
    return result.reshape(angles_all, rows_here, det)


def solution(mesh):
    in_specs = (
        P("angle", None, "row", None),
        P("angle", None),
        P(),
        P(None, ("row", "angle"), None),
    )
    out_specs = P(None, ("row", "angle"), None)
    return jax.shard_map(local, mesh=mesh, in_specs=in_specs, out_specs=out_specs, check_vma=False)
```

```python
import math

import jax
import jax.numpy as jnp
import ml_dtypes
import numpy as np
from jax import lax
from jax.experimental import pallas as pl
from jax.experimental.pallas import tpu as pltpu
from jax.sharding import PartitionSpec as P

WIDTH = 256
LANES = 128


def circulant_blocks(padlen):
    count = padlen // WIDTH
    n = np.arange(padlen, dtype=np.float64)
    odd = np.arange(padlen) % 2 == 1
    taps = np.where(odd, (2.0 / padlen) / np.tan(np.pi * np.where(odd, n, 1.0) / padlen), 0.0)
    m = np.arange(count)[:, None, None]
    p = np.arange(WIDTH)[None, :, None]
    q = np.arange(WIDTH)[None, None, :]
    blocks = taps[(WIDTH * m + q - p) % padlen]
    reverse = -np.eye(WIDTH)[::-1][None]
    return np.concatenate([blocks, reverse], axis=0).astype(ml_dtypes.bfloat16)


def loop(start, stop, body):
    if stop - start <= 8:
        for i in range(start, stop):
            body(i)
    else:
        lax.fori_loop(start, stop, lambda i, _: body(i), None)


def kernel(
    angles, blocks_row, raw_hbm, step_ref, partner_ref, flat_ref, table_hbm, out_ref,
    raw, table, corr, halo, smooth, recv, stage, mirror, ring,
    local_sem, halo_send, halo_recv, send_sem, recv_sem,
):
    steps, rows, det = raw.shape
    chunks = det // LANES
    own = det // WIDTH
    me = lax.axis_index("angle")
    row = lax.axis_index("row")
    after = lax.rem(row + 1, blocks_row)
    before = lax.rem(row + blocks_row - 1, blocks_row)

    barrier = pltpu.get_barrier_semaphore()

    def greet(k):
        pl.semaphore_signal(barrier, inc=1, device_id={"angle": lax.rem(me + k, angles)})

    raw_copy = pltpu.make_async_copy(raw_hbm.at[0], raw, local_sem.at[0])
    raw_copy.start()
    pl.semaphore_signal(barrier, inc=1, device_id={"row": after})
    pl.semaphore_signal(barrier, inc=1, device_id={"row": before})
    loop(1, angles, greet)
    table_copy = pltpu.make_async_copy(table_hbm, table, local_sem.at[1])
    table_copy.start()

    def weight(k, values):
        index = step_ref[0, k]
        value = jnp.float32(values[0])
        for i in range(1, steps):
            value = jnp.where(index == i, jnp.float32(values[i]), value)
        return value

    grid = 2.0 * math.pi * np.arange(steps) / steps
    cosines = [weight(k, np.cos(grid).astype(np.float32)) for k in range(steps)]
    sines = [weight(k, np.sin(grid).astype(np.float32)) for k in range(steps)]
    raw_copy.wait()

    def correlate(g):
        at = g * 8 if isinstance(g, int) else pl.multiple_of(g * 8, 8)
        for c in range(chunks):
            sums = [None, None, None]
            for k in range(steps):
                frame = raw[k, pl.ds(at, 8), c * LANES : (c + 1) * LANES].astype(jnp.float32)
                terms = [frame * cosines[k], frame * sines[k], frame]
                sums = terms if k == 0 else [s + t for s, t in zip(sums, terms)]
            for q in range(3):
                corr[q, pl.ds(at * chunks + c, 8, stride=chunks), :] = sums[q]

    loop(0, rows // 8, correlate)

    pl.semaphore_wait(barrier, angles + 1)

    def halo_copy(side, first, target):
        return pltpu.make_async_remote_copy(
            src_ref=corr.at[:, pl.ds(first * chunks, chunks), :],
            dst_ref=halo.at[side],
            send_sem=halo_send.at[side],
            recv_sem=halo_recv.at[side],
            device_id={"row": target},
        )

    low = halo_copy(0, rows - 1, after)
    high = halo_copy(1, 0, before)
    low.start()
    high.start()

    def line(q, i):
        at = i * chunks if isinstance(i, int) else pl.multiple_of(i * chunks, chunks)
        return corr[q, pl.ds(at, chunks), :]

    def interior(i):
        for q in range(3):
            value = 0.25 * line(q, i - 1) + 0.5 * line(q, i) + 0.25 * line(q, i + 1)
            smooth[i, q] = value.astype(jnp.bfloat16)

    loop(1, rows - 1, interior)

    def row_copy(target):
        return pltpu.make_async_remote_copy(
            src_ref=smooth.at[target],
            dst_ref=recv.at[me],
            send_sem=send_sem.at[target],
            recv_sem=recv_sem.at[me],
            device_id={"angle": target},
        )

    def send_interior(k):
        target = lax.rem(me + k, angles)

        @pl.when((target != 0) & (target != angles - 1))
        def _():
            row_copy(target).start()

    loop(1, angles, send_interior)

    low.wait_recv()
    high.wait_recv()
    for q in range(3):
        edge = jnp.where(row == 0, 0.0, halo[0, q])
        value = 0.25 * edge + 0.5 * line(q, 0) + 0.25 * line(q, 1)
        smooth[0, q] = value.astype(jnp.bfloat16)
    for q in range(3):
        edge = jnp.where(row == blocks_row - 1, 0.0, halo[1, q])
        value = 0.25 * line(q, rows - 2) + 0.5 * line(q, rows - 1) + 0.25 * edge
        smooth[rows - 1, q] = value.astype(jnp.bfloat16)
    for target in (0, angles - 1):
        @pl.when(target != me)
        def _():
            row_copy(target).start()

    recv[me] = smooth[me]
    table_copy.wait()

    def arrived(k):
        source = lax.rem(me + angles - k, angles)
        pltpu.make_async_remote_copy(
            src_ref=smooth.at[source],
            dst_ref=recv.at[source],
            send_sem=send_sem.at[source],
            recv_sem=recv_sem.at[source],
            device_id={"angle": source},
        ).wait_recv()

    loop(1, angles, arrived)

    def spread(a):
        other = partner_ref[a]
        for q in range(3):
            at = a * chunks if isinstance(a, int) else pl.multiple_of(a * chunks, chunks)
            stage[q, pl.ds(at, chunks), :] = recv[a, q].astype(jnp.float32)
            stage[q, pl.ds(at + angles * chunks, chunks), :] = recv[other, q].astype(jnp.float32)

    loop(0, angles, spread)

    flat_cos = flat_ref[0].astype(jnp.float32)
    flat_sin = flat_ref[1].astype(jnp.float32)
    for c in range(chunks):
        lanes = slice(c * LANES, (c + 1) * LANES)
        part = [stage[q, pl.ds(c, 2 * angles, stride=chunks), :] for q in range(3)]
        value = steps * (part[1] * flat_cos[:, lanes] - part[0] * flat_sin[:, lanes]) / part[2]
        dpc = value.astype(jnp.bfloat16).astype(jnp.float32)
        block = c // (WIDTH // LANES)
        at = (c % (WIDTH // LANES)) * LANES
        ring[(own + block) * angles : (own + block + 1) * angles, at : at + LANES] = dpc[:angles]
        back = own - 1 - block
        mirror[back * angles : (back + 1) * angles, at : at + LANES] = dpc[angles:]

    turns = 2 * own
    flipped = jnp.dot(
        mirror[...].astype(jnp.bfloat16), table[turns], preferred_element_type=jnp.float32
    )
    ring[: own * angles] = flipped
    ring[turns * angles : (turns + own) * angles] = flipped

    total = jnp.zeros((own * angles, WIDTH), jnp.float32)
    for m in range(turns):
        first = (own - m) % turns
        window = ring[first * angles : (first + own) * angles].astype(jnp.bfloat16)
        total = total + jnp.dot(window, table[m], preferred_element_type=jnp.float32)
    for block in range(own):
        out_ref[:, block * WIDTH : (block + 1) * WIDTH] = total[
            block * angles : (block + 1) * angles
        ].astype(jnp.bfloat16)

    def sent(k):
        row_copy(lax.rem(me + k, angles)).wait_send()

    loop(1, angles, sent)
    low.wait_send()
    high.wait_send()


def local(raw_frames, step_index, partner, flat_field):
    _, steps, rows, det = raw_frames.shape
    angles = lax.axis_size("angle")
    blocks_row = lax.axis_size("row")
    chunks = det // LANES
    own = det // WIDTH
    assert rows == angles and rows % 8 == 0 and raw_frames.shape[0] == 1
    table = jnp.asarray(circulant_blocks(2 * det))
    body = lambda *refs: kernel(angles, blocks_row, *refs)
    result = pl.pallas_call(
        body,
        out_shape=jax.ShapeDtypeStruct((angles, det), jnp.bfloat16),
        in_specs=[
            pl.BlockSpec(memory_space=pl.ANY),
            pl.BlockSpec(memory_space=pltpu.SMEM),
            pl.BlockSpec(memory_space=pltpu.SMEM),
            pl.BlockSpec(memory_space=pltpu.VMEM),
            pl.BlockSpec(memory_space=pl.ANY),
        ],
        out_specs=pl.BlockSpec(memory_space=pltpu.VMEM),
        scratch_shapes=[
            pltpu.VMEM((steps, rows, det), jnp.bfloat16),
            pltpu.VMEM(table.shape, jnp.bfloat16),
            pltpu.VMEM((3, rows * chunks, LANES), jnp.float32),
            pltpu.VMEM((2, 3, chunks, LANES), jnp.float32),
            pltpu.VMEM((rows, 3, chunks, LANES), jnp.bfloat16),
            pltpu.VMEM((angles, 3, chunks, LANES), jnp.bfloat16),
            pltpu.VMEM((3, 2 * angles * chunks, LANES), jnp.float32),
            pltpu.VMEM((own * angles, WIDTH), jnp.float32),
            pltpu.VMEM((3 * own * angles, WIDTH), jnp.float32),
            pltpu.SemaphoreType.DMA((2,)),
            pltpu.SemaphoreType.DMA((2,)),
            pltpu.SemaphoreType.DMA((2,)),
            pltpu.SemaphoreType.DMA((angles,)),
            pltpu.SemaphoreType.DMA((angles,)),
        ],
        compiler_params=pltpu.CompilerParams(
            collective_id=0, has_side_effects=True, vmem_limit_bytes=48 * 1024 * 1024
        ),
    )(raw_frames, step_index, partner, flat_field, table)
    return result[:, None, :]


def solution(mesh):
    in_specs = (
        P("angle", None, "row", None),
        P("angle", None),
        P(),
        P(None, ("row", "angle"), None),
    )
    out_specs = P(None, ("row", "angle"), None)
    return jax.shard_map(local, mesh=mesh, in_specs=in_specs, out_specs=out_specs, check_vma=False)
```

```python
import math

import jax
import jax.numpy as jnp
import ml_dtypes
import numpy as np
from jax import lax
from jax.experimental import pallas as pl
from jax.experimental.pallas import tpu as pltpu
from jax.sharding import PartitionSpec as P

WIDTH = 256
LANES = 128


def circulant_blocks(padlen):
    count = padlen // WIDTH
    n = np.arange(padlen, dtype=np.float64)
    odd = np.arange(padlen) % 2 == 1
    taps = np.where(odd, (2.0 / padlen) / np.tan(np.pi * np.where(odd, n, 1.0) / padlen), 0.0)
    m = np.arange(count)[:, None, None]
    p = np.arange(WIDTH)[None, :, None]
    q = np.arange(WIDTH)[None, None, :]
    blocks = taps[(WIDTH * m + q - p) % padlen]
    reverse = -np.eye(WIDTH)[::-1][None]
    return np.concatenate([blocks, reverse], axis=0).astype(ml_dtypes.bfloat16)


def loop(start, stop, body):
    if stop - start <= 8:
        for i in range(start, stop):
            body(i)
    else:
        lax.fori_loop(start, stop, lambda i, _: body(i), None)


def kernel(
    angles, blocks_row, raw_hbm, step_hbm, partner_hbm, flat_hbm, table_hbm, out_ref,
    raw, table, step_ref, partner_ref, flat_ref, corr, halo, smooth, recv, stage, mirror, ring,
    local_sem, halo_send, halo_recv, send_sem, recv_sem,
):
    steps, rows, det = raw.shape
    chunks = det // LANES
    own = det // WIDTH
    me = lax.axis_index("angle")
    row = lax.axis_index("row")
    after = lax.rem(row + 1, blocks_row)
    before = lax.rem(row + blocks_row - 1, blocks_row)

    barrier = pltpu.get_barrier_semaphore()

    def greet(k):
        pl.semaphore_signal(barrier, inc=1, device_id={"angle": lax.rem(me + k, angles)})

    raw_copy = pltpu.make_async_copy(raw_hbm.at[0], raw, local_sem.at[0])
    raw_copy.start()
    step_copy = pltpu.make_async_copy(step_hbm, step_ref, local_sem.at[2])
    step_copy.start()
    pl.semaphore_signal(barrier, inc=1, device_id={"row": after})
    pl.semaphore_signal(barrier, inc=1, device_id={"row": before})
    loop(1, angles, greet)
    table_copy = pltpu.make_async_copy(table_hbm, table, local_sem.at[1])
    table_copy.start()
    partner_copy = pltpu.make_async_copy(partner_hbm, partner_ref, local_sem.at[3])
    partner_copy.start()
    flat_copy = pltpu.make_async_copy(flat_hbm, flat_ref, local_sem.at[4])
    flat_copy.start()
    step_copy.wait()

    def weight(k, values):
        index = step_ref[0, k]
        value = jnp.float32(values[0])
        for i in range(1, steps):
            value = jnp.where(index == i, jnp.float32(values[i]), value)
        return value

    grid = 2.0 * math.pi * np.arange(steps) / steps
    cosines = [weight(k, np.cos(grid).astype(np.float32)) for k in range(steps)]
    sines = [weight(k, np.sin(grid).astype(np.float32)) for k in range(steps)]
    raw_copy.wait()

    def correlate(g):
        at = g * 8 if isinstance(g, int) else pl.multiple_of(g * 8, 8)
        for c in range(chunks):
            sums = [None, None, None]
            for k in range(steps):
                frame = raw[k, pl.ds(at, 8), c * LANES : (c + 1) * LANES].astype(jnp.float32)
                terms = [frame * cosines[k], frame * sines[k], frame]
                sums = terms if k == 0 else [s + t for s, t in zip(sums, terms)]
            for q in range(3):
                corr[q, pl.ds(at * chunks + c, 8, stride=chunks), :] = sums[q]

    loop(0, rows // 8, correlate)

    pl.semaphore_wait(barrier, angles + 1)

    def halo_copy(side, first, target):
        return pltpu.make_async_remote_copy(
            src_ref=corr.at[:, pl.ds(first * chunks, chunks), :],
            dst_ref=halo.at[side],
            send_sem=halo_send.at[side],
            recv_sem=halo_recv.at[side],
            device_id={"row": target},
        )

    low = halo_copy(0, rows - 1, after)
    high = halo_copy(1, 0, before)
    low.start()
    high.start()

    def line(q, i):
        at = i * chunks if isinstance(i, int) else pl.multiple_of(i * chunks, chunks)
        return corr[q, pl.ds(at, chunks), :]

    def interior(i):
        for q in range(3):
            value = 0.25 * line(q, i - 1) + 0.5 * line(q, i) + 0.25 * line(q, i + 1)
            smooth[i, q] = value.astype(jnp.bfloat16)

    loop(1, rows - 1, interior)

    def row_copy(target):
        return pltpu.make_async_remote_copy(
            src_ref=smooth.at[target],
            dst_ref=recv.at[me],
            send_sem=send_sem.at[target],
            recv_sem=recv_sem.at[me],
            device_id={"angle": target},
        )

    def send_interior(k):
        target = lax.rem(me + k, angles)

        @pl.when((target != 0) & (target != angles - 1))
        def _():
            row_copy(target).start()

    loop(1, angles, send_interior)

    low.wait_recv()
    high.wait_recv()
    for q in range(3):
        edge = jnp.where(row == 0, 0.0, halo[0, q])
        value = 0.25 * edge + 0.5 * line(q, 0) + 0.25 * line(q, 1)
        smooth[0, q] = value.astype(jnp.bfloat16)
    for q in range(3):
        edge = jnp.where(row == blocks_row - 1, 0.0, halo[1, q])
        value = 0.25 * line(q, rows - 2) + 0.5 * line(q, rows - 1) + 0.25 * edge
        smooth[rows - 1, q] = value.astype(jnp.bfloat16)
    for target in (0, angles - 1):
        @pl.when(target != me)
        def _():
            row_copy(target).start()

    recv[me] = smooth[me]
    table_copy.wait()
    partner_copy.wait()
    flat_copy.wait()

    def arrived(k):
        source = lax.rem(me + angles - k, angles)
        pltpu.make_async_remote_copy(
            src_ref=smooth.at[source],
            dst_ref=recv.at[source],
            send_sem=send_sem.at[source],
            recv_sem=recv_sem.at[source],
            device_id={"angle": source},
        ).wait_recv()

    loop(1, angles, arrived)

    def spread(a):
        other = partner_ref[a]
        for q in range(3):
            at = a * chunks if isinstance(a, int) else pl.multiple_of(a * chunks, chunks)
            stage[q, pl.ds(at, chunks), :] = recv[a, q].astype(jnp.float32)
            stage[q, pl.ds(at + angles * chunks, chunks), :] = recv[other, q].astype(jnp.float32)

    loop(0, angles, spread)

    flat = flat_ref[...].astype(jnp.float32)
    flat_cos, flat_sin = flat[0:1], flat[1:2]
    for c in range(chunks):
        lanes = slice(c * LANES, (c + 1) * LANES)
        part = [stage[q, pl.ds(c, 2 * angles, stride=chunks), :] for q in range(3)]
        value = steps * (part[1] * flat_cos[:, lanes] - part[0] * flat_sin[:, lanes]) / part[2]
        dpc = value.astype(jnp.bfloat16).astype(jnp.float32)
        block = c // (WIDTH // LANES)
        at = (c % (WIDTH // LANES)) * LANES
        ring[(own + block) * angles : (own + block + 1) * angles, at : at + LANES] = dpc[:angles]
        back = own - 1 - block
        mirror[back * angles : (back + 1) * angles, at : at + LANES] = dpc[angles:]

    turns = 2 * own
    flipped = jnp.dot(
        mirror[...].astype(jnp.bfloat16), table[turns], preferred_element_type=jnp.float32
    )
    ring[: own * angles] = flipped
    ring[turns * angles : (turns + own) * angles] = flipped

    total = jnp.zeros((own * angles, WIDTH), jnp.float32)
    for m in range(turns):
        first = (own - m) % turns
        window = ring[first * angles : (first + own) * angles].astype(jnp.bfloat16)
        total = total + jnp.dot(window, table[m], preferred_element_type=jnp.float32)
    for block in range(own):
        out_ref[:, block * WIDTH : (block + 1) * WIDTH] = total[
            block * angles : (block + 1) * angles
        ].astype(jnp.bfloat16)

    def sent(k):
        row_copy(lax.rem(me + k, angles)).wait_send()

    loop(1, angles, sent)
    low.wait_send()
    high.wait_send()


def local(raw_frames, step_index, partner, flat_field):
    _, steps, rows, det = raw_frames.shape
    angles = lax.axis_size("angle")
    blocks_row = lax.axis_size("row")
    chunks = det // LANES
    own = det // WIDTH
    assert rows == angles and rows % 8 == 0 and raw_frames.shape[0] == 1
    table = jnp.asarray(circulant_blocks(2 * det))
    body = lambda *refs: kernel(angles, blocks_row, *refs)
    result = pl.pallas_call(
        body,
        out_shape=jax.ShapeDtypeStruct((angles, det), jnp.bfloat16),
        in_specs=[pl.BlockSpec(memory_space=pltpu.HBM)] * 5,
        out_specs=pl.BlockSpec(memory_space=pltpu.VMEM),
        scratch_shapes=[
            pltpu.VMEM((steps, rows, det), jnp.bfloat16),
            pltpu.VMEM(table.shape, jnp.bfloat16),
            pltpu.SMEM((1, steps), jnp.int32),
            pltpu.SMEM((angles,), jnp.int32),
            pltpu.VMEM((2, det), jnp.bfloat16),
            pltpu.VMEM((3, rows * chunks, LANES), jnp.float32),
            pltpu.VMEM((2, 3, chunks, LANES), jnp.float32),
            pltpu.VMEM((rows, 3, chunks, LANES), jnp.bfloat16),
            pltpu.VMEM((angles, 3, chunks, LANES), jnp.bfloat16),
            pltpu.VMEM((3, 2 * angles * chunks, LANES), jnp.float32),
            pltpu.VMEM((own * angles, WIDTH), jnp.float32),
            pltpu.VMEM((3 * own * angles, WIDTH), jnp.float32),
            pltpu.SemaphoreType.DMA((5,)),
            pltpu.SemaphoreType.DMA((2,)),
            pltpu.SemaphoreType.DMA((2,)),
            pltpu.SemaphoreType.DMA((angles,)),
            pltpu.SemaphoreType.DMA((angles,)),
        ],
        compiler_params=pltpu.CompilerParams(
            collective_id=0, has_side_effects=True, vmem_limit_bytes=48 * 1024 * 1024
        ),
    )(raw_frames, step_index, partner, flat_field[:, 0, :], table)
    return result[:, None, :]


def solution(mesh):
    in_specs = (
        P("angle", None, "row", None),
        P("angle", None),
        P(),
        P(None, ("row", "angle"), None),
    )
    out_specs = P(None, ("row", "angle"), None)
    return jax.shard_map(local, mesh=mesh, in_specs=in_specs, out_specs=out_specs, check_vma=False)
```

```python
import math

import jax
import jax.numpy as jnp
import ml_dtypes
import numpy as np
from jax import lax
from jax.experimental import pallas as pl
from jax.experimental.pallas import tpu as pltpu
from jax.sharding import PartitionSpec as P

WIDTH = 256
LANES = 128


def circulant_blocks(padlen):
    count = padlen // WIDTH
    n = np.arange(padlen, dtype=np.float64)
    odd = np.arange(padlen) % 2 == 1
    taps = np.where(odd, (2.0 / padlen) / np.tan(np.pi * np.where(odd, n, 1.0) / padlen), 0.0)
    m = np.arange(count)[:, None, None]
    p = np.arange(WIDTH)[None, :, None]
    q = np.arange(WIDTH)[None, None, :]
    blocks = taps[(WIDTH * m + q - p) % padlen]
    reverse = -np.eye(WIDTH)[::-1][None]
    return np.concatenate([blocks, reverse], axis=0).astype(ml_dtypes.bfloat16)


def loop(start, stop, body):
    if stop - start <= 8:
        for i in range(start, stop):
            body(i)
    else:
        lax.fori_loop(start, stop, lambda i, _: body(i), None)


def kernel(
    angles, blocks_row, raw_hbm, step_hbm, partner_hbm, flat_hbm, table_hbm, out_ref,
    raw, table, step_ref, partner_ref, flat_ref, corr, halo, smooth, recv, stage, mirror, ring,
    local_sem, halo_send, halo_recv, send_sem, recv_sem,
):
    steps, rows, det = raw.shape
    chunks = det // LANES
    own = det // WIDTH
    me = lax.axis_index("angle")
    row = lax.axis_index("row")
    after = lax.rem(row + 1, blocks_row)
    before = lax.rem(row + blocks_row - 1, blocks_row)

    barrier = pltpu.get_barrier_semaphore()

    def greet(k):
        pl.semaphore_signal(barrier, inc=1, device_id={"angle": lax.rem(me + k, angles)})

    raw_copy = pltpu.make_async_copy(raw_hbm.at[0], raw, local_sem.at[0])
    raw_copy.start()
    step_copy = pltpu.make_async_copy(step_hbm, step_ref, local_sem.at[2])
    step_copy.start()
    pl.semaphore_signal(barrier, inc=1, device_id={"row": after})
    pl.semaphore_signal(barrier, inc=1, device_id={"row": before})
    loop(1, angles, greet)
    table_copy = pltpu.make_async_copy(table_hbm, table, local_sem.at[1])
    table_copy.start()
    partner_copy = pltpu.make_async_copy(partner_hbm, partner_ref, local_sem.at[3])
    partner_copy.start()
    flat_copy = pltpu.make_async_copy(flat_hbm, flat_ref, local_sem.at[4])
    flat_copy.start()
    step_copy.wait()

    def weight(k, values):
        index = step_ref[0, k]
        value = jnp.float32(values[0])
        for i in range(1, steps):
            value = jnp.where(index == i, jnp.float32(values[i]), value)
        return value

    grid = 2.0 * math.pi * np.arange(steps) / steps
    cosines = [weight(k, np.cos(grid).astype(np.float32)) for k in range(steps)]
    sines = [weight(k, np.sin(grid).astype(np.float32)) for k in range(steps)]
    raw_copy.wait()

    def correlate(g):
        at = g * 8 if isinstance(g, int) else pl.multiple_of(g * 8, 8)
        for c in range(chunks):
            sums = [None, None, None]
            for k in range(steps):
                frame = raw[k, pl.ds(at, 8), c * LANES : (c + 1) * LANES].astype(jnp.float32)
                terms = [frame * cosines[k], frame * sines[k], frame]
                sums = terms if k == 0 else [s + t for s, t in zip(sums, terms)]
            for q in range(3):
                corr[q, pl.ds(at * chunks + c, 8, stride=chunks), :] = sums[q]

    loop(0, rows // 8, correlate)

    pl.semaphore_wait(barrier, angles + 1)

    def halo_copy(side, first, target):
        return pltpu.make_async_remote_copy(
            src_ref=corr.at[:, pl.ds(first * chunks, chunks), :],
            dst_ref=halo.at[side],
            send_sem=halo_send.at[side],
            recv_sem=halo_recv.at[side],
            device_id={"row": target},
        )

    low = halo_copy(0, rows - 1, after)
    high = halo_copy(1, 0, before)
    low.start()
    high.start()

    def line(q, i):
        at = i * chunks if isinstance(i, int) else pl.multiple_of(i * chunks, chunks)
        return corr[q, pl.ds(at, chunks), :]

    def interior(i):
        for q in range(3):
            value = 0.25 * line(q, i - 1) + 0.5 * line(q, i) + 0.25 * line(q, i + 1)
            smooth[i, q] = value.astype(jnp.bfloat16)

    loop(1, rows - 1, interior)

    def row_copy(target):
        return pltpu.make_async_remote_copy(
            src_ref=smooth.at[target],
            dst_ref=recv.at[me],
            send_sem=send_sem.at[target],
            recv_sem=recv_sem.at[me],
            device_id={"angle": target},
        )

    def send_interior(k):
        target = lax.rem(me + k, angles)

        @pl.when((target != 0) & (target != angles - 1))
        def _():
            row_copy(target).start()

    loop(1, angles, send_interior)

    low.wait_recv()
    high.wait_recv()
    for q in range(3):
        edge = jnp.where(row == 0, 0.0, halo[0, q])
        value = 0.25 * edge + 0.5 * line(q, 0) + 0.25 * line(q, 1)
        smooth[0, q] = value.astype(jnp.bfloat16)
    for q in range(3):
        edge = jnp.where(row == blocks_row - 1, 0.0, halo[1, q])
        value = 0.25 * line(q, rows - 2) + 0.5 * line(q, rows - 1) + 0.25 * edge
        smooth[rows - 1, q] = value.astype(jnp.bfloat16)
    for target in (0, angles - 1):
        @pl.when(target != me)
        def _():
            row_copy(target).start()

    recv[me] = smooth[me]
    table_copy.wait()
    partner_copy.wait()
    flat_copy.wait()

    def arrived(k):
        source = lax.rem(me + angles - k, angles)
        pltpu.make_async_remote_copy(
            src_ref=smooth.at[source],
            dst_ref=recv.at[source],
            send_sem=send_sem.at[source],
            recv_sem=recv_sem.at[source],
            device_id={"angle": source},
        ).wait_recv()

    loop(1, angles, arrived)

    def spread(a):
        other = partner_ref[a]
        for q in range(3):
            at = a * chunks if isinstance(a, int) else pl.multiple_of(a * chunks, chunks)
            stage[q, pl.ds(at, chunks), :] = recv[a, q].astype(jnp.float32)
            stage[q, pl.ds(at + angles * chunks, chunks), :] = recv[other, q].astype(jnp.float32)

    loop(0, angles, spread)

    flat = flat_ref[...].astype(jnp.float32)
    flat_cos, flat_sin = flat[0:1], flat[1:2]
    for c in range(chunks):
        lanes = slice(c * LANES, (c + 1) * LANES)
        part = [stage[q, pl.ds(c, 2 * angles, stride=chunks), :] for q in range(3)]
        value = steps * (part[1] * flat_cos[:, lanes] - part[0] * flat_sin[:, lanes]) / part[2]
        dpc = value.astype(jnp.bfloat16).astype(jnp.float32)
        block = c // (WIDTH // LANES)
        at = (c % (WIDTH // LANES)) * LANES
        ring[(own + block) * angles : (own + block + 1) * angles, at : at + LANES] = dpc[:angles]
        back = own - 1 - block
        mirror[back * angles : (back + 1) * angles, at : at + LANES] = dpc[angles:]

    turns = 2 * own
    flipped = jnp.dot(
        mirror[...].astype(jnp.bfloat16), table[turns], preferred_element_type=jnp.float32
    )
    ring[: own * angles] = flipped
    ring[turns * angles : (turns + own) * angles] = flipped

    total = jnp.zeros((own * angles, WIDTH), jnp.float32)
    for m in range(turns):
        first = (own - m) % turns
        window = ring[first * angles : (first + own) * angles].astype(jnp.bfloat16)
        total = total + jnp.dot(window, table[m], preferred_element_type=jnp.float32)
    for block in range(own):
        out_ref[:, block * WIDTH : (block + 1) * WIDTH] = total[
            block * angles : (block + 1) * angles
        ].astype(jnp.bfloat16)

    def sent(k):
        row_copy(lax.rem(me + k, angles)).wait_send()

    loop(1, angles, sent)
    low.wait_send()
    high.wait_send()


def local(raw_frames, step_index, partner, flat_field):
    _, steps, rows, det = raw_frames.shape
    angles = lax.axis_size("angle")
    blocks_row = lax.axis_size("row")
    chunks = det // LANES
    own = det // WIDTH
    assert rows == angles and rows % 8 == 0 and raw_frames.shape[0] == 1
    table = jnp.asarray(circulant_blocks(2 * det))
    body = lambda *refs: kernel(angles, blocks_row, *refs)
    result = pl.pallas_call(
        body,
        out_shape=jax.ShapeDtypeStruct((angles, det), jnp.bfloat16),
        in_specs=[pl.BlockSpec(memory_space=pltpu.HBM)] * 5,
        out_specs=pl.BlockSpec(memory_space=pltpu.VMEM),
        scratch_shapes=[
            pltpu.VMEM((steps, rows, det), jnp.bfloat16),
            pltpu.VMEM(table.shape, jnp.bfloat16),
            pltpu.SMEM((1, steps), jnp.int32),
            pltpu.SMEM((angles,), jnp.int32),
            pltpu.VMEM((2, det), jnp.bfloat16),
            pltpu.VMEM((3, rows * chunks, LANES), jnp.float32),
            pltpu.VMEM((2, 3, chunks, LANES), jnp.float32),
            pltpu.VMEM((rows, 3, chunks, LANES), jnp.bfloat16),
            pltpu.VMEM((angles, 3, chunks, LANES), jnp.bfloat16),
            pltpu.VMEM((3, 2 * angles * chunks, LANES), jnp.float32),
            pltpu.VMEM((own * angles, WIDTH), jnp.float32),
            pltpu.VMEM((3 * own * angles, WIDTH), jnp.float32),
            pltpu.SemaphoreType.DMA((5,)),
            pltpu.SemaphoreType.DMA((2,)),
            pltpu.SemaphoreType.DMA((2,)),
            pltpu.SemaphoreType.DMA((angles,)),
            pltpu.SemaphoreType.DMA((angles,)),
        ],
        compiler_params=pltpu.CompilerParams(
            collective_id=0, has_side_effects=True, vmem_limit_bytes=48 * 1024 * 1024
        ),
    )(*[pltpu.with_memory_space_constraint(x, pltpu.HBM) for x in (raw_frames, step_index, partner, flat_field[:, 0, :], table)])
    return result[:, None, :]


def solution(mesh):
    in_specs = (
        P("angle", None, "row", None),
        P("angle", None),
        P(),
        P(None, ("row", "angle"), None),
    )
    out_specs = P(None, ("row", "angle"), None)
    return jax.shard_map(local, mesh=mesh, in_specs=in_specs, out_specs=out_specs, check_vma=False)
```

```python
import math

import jax
import jax.numpy as jnp
import ml_dtypes
import numpy as np
from jax import lax
from jax.experimental import pallas as pl
from jax.experimental.pallas import tpu as pltpu
from jax.sharding import PartitionSpec as P

WIDTH = 256
LANES = 128


def circulant_blocks(padlen):
    count = padlen // WIDTH
    n = np.arange(padlen, dtype=np.float64)
    odd = np.arange(padlen) % 2 == 1
    taps = np.where(odd, (2.0 / padlen) / np.tan(np.pi * np.where(odd, n, 1.0) / padlen), 0.0)
    m = np.arange(count)[:, None, None]
    p = np.arange(WIDTH)[None, :, None]
    q = np.arange(WIDTH)[None, None, :]
    blocks = taps[(WIDTH * m + q - p) % padlen]
    reverse = -np.eye(WIDTH)[::-1][None]
    return np.concatenate([blocks, reverse], axis=0).astype(ml_dtypes.bfloat16)


def loop(start, stop, body):
    if stop - start <= 8:
        for i in range(start, stop):
            body(i)
    else:
        lax.fori_loop(start, stop, lambda i, _: body(i), None)


def kernel(
    angles, blocks_row, raw_hbm, step_hbm, partner_hbm, flat_hbm, table_hbm, out_ref,
    raw, table, step_ref, partner_ref, flat_ref, corr, halo, smooth, recv, stage, mirror, ring,
    local_sem, halo_send, halo_recv, send_sem, recv_sem,
):
    steps, rows, det = raw.shape
    chunks = det // LANES
    own = det // WIDTH
    me = lax.axis_index("angle")
    row = lax.axis_index("row")
    after = lax.rem(row + 1, blocks_row)
    before = lax.rem(row + blocks_row - 1, blocks_row)

    barrier = pltpu.get_barrier_semaphore()

    def greet(k):
        pl.semaphore_signal(barrier, inc=1, device_id={"angle": lax.rem(me + k, angles)})

    raw_copy = pltpu.make_async_copy(raw_hbm.at[0], raw, local_sem.at[0])
    raw_copy.start()
    step_copy = pltpu.make_async_copy(step_hbm, step_ref, local_sem.at[2])
    step_copy.start()
    has_before = row > 0
    has_after = row < blocks_row - 1

    loop(1, angles, greet)

    @pl.when(has_after)
    def _():
        pl.semaphore_signal(barrier, inc=1, device_id={"row": after})

    @pl.when(has_before)
    def _():
        pl.semaphore_signal(barrier, inc=1, device_id={"row": before})

    @pl.when(row == 0)
    def _():
        halo[0] = jnp.zeros_like(halo[0])

    @pl.when(row == blocks_row - 1)
    def _():
        halo[1] = jnp.zeros_like(halo[1])

    table_copy = pltpu.make_async_copy(table_hbm, table, local_sem.at[1])
    table_copy.start()
    partner_copy = pltpu.make_async_copy(partner_hbm, partner_ref, local_sem.at[3])
    partner_copy.start()
    flat_copy = pltpu.make_async_copy(flat_hbm, flat_ref, local_sem.at[4])
    flat_copy.start()
    step_copy.wait()

    def weight(k, values):
        index = step_ref[0, k]
        value = jnp.float32(values[0])
        for i in range(1, steps):
            value = jnp.where(index == i, jnp.float32(values[i]), value)
        return value

    grid = 2.0 * math.pi * np.arange(steps) / steps
    cosines = [weight(k, np.cos(grid).astype(np.float32)) for k in range(steps)]
    sines = [weight(k, np.sin(grid).astype(np.float32)) for k in range(steps)]
    raw_copy.wait()

    def correlate(g):
        at = g * 8 if isinstance(g, int) else pl.multiple_of(g * 8, 8)
        for c in range(chunks):
            sums = [None, None, None]
            for k in range(steps):
                frame = raw[k, pl.ds(at, 8), c * LANES : (c + 1) * LANES].astype(jnp.float32)
                terms = [frame * cosines[k], frame * sines[k], frame]
                sums = terms if k == 0 else [s + t for s, t in zip(sums, terms)]
            for q in range(3):
                corr[q, pl.ds(at * chunks + c, 8, stride=chunks), :] = sums[q]

    loop(0, rows // 8, correlate)

    pl.semaphore_wait(
        barrier, angles - 1 + has_before.astype(jnp.int32) + has_after.astype(jnp.int32)
    )

    def halo_copy(side, first, target):
        return pltpu.make_async_remote_copy(
            src_ref=corr.at[:, pl.ds(first * chunks, chunks), :],
            dst_ref=halo.at[side],
            send_sem=halo_send.at[side],
            recv_sem=halo_recv.at[side],
            device_id={"row": target},
        )

    low = halo_copy(0, rows - 1, after)
    high = halo_copy(1, 0, before)

    @pl.when(has_after)
    def _():
        low.start()

    @pl.when(has_before)
    def _():
        high.start()

    def line(q, i):
        at = i * chunks if isinstance(i, int) else pl.multiple_of(i * chunks, chunks)
        return corr[q, pl.ds(at, chunks), :]

    def interior(i):
        for q in range(3):
            value = 0.25 * line(q, i - 1) + 0.5 * line(q, i) + 0.25 * line(q, i + 1)
            smooth[i, q] = value.astype(jnp.bfloat16)

    loop(1, rows - 1, interior)

    def row_copy(target):
        return pltpu.make_async_remote_copy(
            src_ref=smooth.at[target],
            dst_ref=recv.at[me],
            send_sem=send_sem.at[target],
            recv_sem=recv_sem.at[me],
            device_id={"angle": target},
        )

    def send(target):
        @pl.when(target != me)
        def _():
            row_copy(target).start()

    @pl.when(has_before)
    def _():
        low.wait_recv()

    for q in range(3):
        value = 0.25 * halo[0, q] + 0.5 * line(q, 0) + 0.25 * line(q, 1)
        smooth[0, q] = value.astype(jnp.bfloat16)
    send(0)
    loop(1, angles - 1, send)

    @pl.when(has_after)
    def _():
        high.wait_recv()

    for q in range(3):
        value = 0.25 * line(q, rows - 2) + 0.5 * line(q, rows - 1) + 0.25 * halo[1, q]
        smooth[rows - 1, q] = value.astype(jnp.bfloat16)
    send(angles - 1)

    recv[me] = smooth[me]
    table_copy.wait()
    partner_copy.wait()
    flat_copy.wait()

    def arrived(k):
        source = lax.rem(me + angles - k, angles)
        pltpu.make_async_remote_copy(
            src_ref=smooth.at[source],
            dst_ref=recv.at[source],
            send_sem=send_sem.at[source],
            recv_sem=recv_sem.at[source],
            device_id={"angle": source},
        ).wait_recv()

    loop(1, angles, arrived)

    def spread(a):
        other = partner_ref[a]
        for q in range(3):
            at = a * chunks if isinstance(a, int) else pl.multiple_of(a * chunks, chunks)
            stage[q, pl.ds(at, chunks), :] = recv[a, q].astype(jnp.float32)
            stage[q, pl.ds(at + angles * chunks, chunks), :] = recv[other, q].astype(jnp.float32)

    loop(0, angles, spread)

    flat = flat_ref[...].astype(jnp.float32)
    flat_cos, flat_sin = flat[0:1], flat[1:2]
    for c in range(chunks):
        lanes = slice(c * LANES, (c + 1) * LANES)
        part = [stage[q, pl.ds(c, 2 * angles, stride=chunks), :] for q in range(3)]
        value = steps * (part[1] * flat_cos[:, lanes] - part[0] * flat_sin[:, lanes]) / part[2]
        dpc = value.astype(jnp.bfloat16).astype(jnp.float32)
        block = c // (WIDTH // LANES)
        at = (c % (WIDTH // LANES)) * LANES
        ring[(own + block) * angles : (own + block + 1) * angles, at : at + LANES] = dpc[:angles]
        back = own - 1 - block
        mirror[back * angles : (back + 1) * angles, at : at + LANES] = dpc[angles:]

    turns = 2 * own
    flipped = jnp.dot(
        mirror[...].astype(jnp.bfloat16), table[turns], preferred_element_type=jnp.float32
    )
    ring[: own * angles] = flipped
    ring[turns * angles : (turns + own) * angles] = flipped

    total = jnp.zeros((own * angles, WIDTH), jnp.float32)
    for m in range(turns):
        first = (own - m) % turns
        window = ring[first * angles : (first + own) * angles].astype(jnp.bfloat16)
        total = total + jnp.dot(window, table[m], preferred_element_type=jnp.float32)
    for block in range(own):
        out_ref[:, block * WIDTH : (block + 1) * WIDTH] = total[
            block * angles : (block + 1) * angles
        ].astype(jnp.bfloat16)

    def sent(k):
        row_copy(lax.rem(me + k, angles)).wait_send()

    loop(1, angles, sent)

    @pl.when(has_after)
    def _():
        low.wait_send()

    @pl.when(has_before)
    def _():
        high.wait_send()


def local(raw_frames, step_index, partner, flat_field):
    _, steps, rows, det = raw_frames.shape
    angles = lax.axis_size("angle")
    blocks_row = lax.axis_size("row")
    chunks = det // LANES
    own = det // WIDTH
    assert rows == angles and rows % 8 == 0 and raw_frames.shape[0] == 1
    table = jnp.asarray(circulant_blocks(2 * det))
    body = lambda *refs: kernel(angles, blocks_row, *refs)
    result = pl.pallas_call(
        body,
        out_shape=jax.ShapeDtypeStruct((angles, det), jnp.bfloat16),
        in_specs=[pl.BlockSpec(memory_space=pltpu.HBM)] * 5,
        out_specs=pl.BlockSpec(memory_space=pltpu.VMEM),
        scratch_shapes=[
            pltpu.VMEM((steps, rows, det), jnp.bfloat16),
            pltpu.VMEM(table.shape, jnp.bfloat16),
            pltpu.SMEM((1, steps), jnp.int32),
            pltpu.SMEM((angles,), jnp.int32),
            pltpu.VMEM((2, det), jnp.bfloat16),
            pltpu.VMEM((3, rows * chunks, LANES), jnp.float32),
            pltpu.VMEM((2, 3, chunks, LANES), jnp.float32),
            pltpu.VMEM((rows, 3, chunks, LANES), jnp.bfloat16),
            pltpu.VMEM((angles, 3, chunks, LANES), jnp.bfloat16),
            pltpu.VMEM((3, 2 * angles * chunks, LANES), jnp.float32),
            pltpu.VMEM((own * angles, WIDTH), jnp.float32),
            pltpu.VMEM((3 * own * angles, WIDTH), jnp.float32),
            pltpu.SemaphoreType.DMA((5,)),
            pltpu.SemaphoreType.DMA((2,)),
            pltpu.SemaphoreType.DMA((2,)),
            pltpu.SemaphoreType.DMA((angles,)),
            pltpu.SemaphoreType.DMA((angles,)),
        ],
        compiler_params=pltpu.CompilerParams(
            collective_id=0, has_side_effects=True, vmem_limit_bytes=48 * 1024 * 1024
        ),
    )(*[pltpu.with_memory_space_constraint(x, pltpu.HBM) for x in (raw_frames, step_index, partner, flat_field[:, 0, :], table)])
    return result[:, None, :]


def solution(mesh):
    in_specs = (
        P("angle", None, "row", None),
        P("angle", None),
        P(),
        P(None, ("row", "angle"), None),
    )
    out_specs = P(None, ("row", "angle"), None)
    return jax.shard_map(local, mesh=mesh, in_specs=in_specs, out_specs=out_specs, check_vma=False)
```

```python
import math

import jax
import jax.numpy as jnp
import ml_dtypes
import numpy as np
from jax import lax
from jax.experimental import pallas as pl
from jax.experimental.pallas import tpu as pltpu
from jax.sharding import PartitionSpec as P

WIDTH = 256
LANES = 128


def circulant_blocks(padlen):
    count = padlen // WIDTH
    n = np.arange(padlen, dtype=np.float64)
    odd = np.arange(padlen) % 2 == 1
    taps = np.where(odd, (2.0 / padlen) / np.tan(np.pi * np.where(odd, n, 1.0) / padlen), 0.0)
    m = np.arange(count)[:, None, None]
    p = np.arange(WIDTH)[None, :, None]
    q = np.arange(WIDTH)[None, None, :]
    blocks = taps[(WIDTH * m + q - p) % padlen]
    reverse = -np.eye(WIDTH)[::-1][None]
    return np.concatenate([blocks, reverse], axis=0).astype(ml_dtypes.bfloat16)


def loop(start, stop, body):
    if stop - start <= 8:
        for i in range(start, stop):
            body(i)
    else:
        lax.fori_loop(start, stop, lambda i, _: body(i), None)


def kernel(
    angles, blocks_row, raw_hbm, step_hbm, partner_hbm, flat_hbm, table_hbm, out_ref,
    raw, table, step_ref, partner_ref, flat_ref, corr, halo, partial, edge, part, extra, smooth, recv, stage, mirror, ring,
    local_sem, halo_send, halo_recv, edge_send, extra_recv, send_sem, recv_sem,
):
    steps, rows, det = raw.shape
    chunks = det // LANES
    own = det // WIDTH
    me = lax.axis_index("angle")
    row = lax.axis_index("row")
    after = lax.rem(row + 1, blocks_row)
    before = lax.rem(row + blocks_row - 1, blocks_row)

    barrier = pltpu.get_barrier_semaphore()

    def greet(k):
        pl.semaphore_signal(barrier, inc=1, device_id={"angle": lax.rem(me + k, angles)})

    raw_copy = pltpu.make_async_copy(raw_hbm.at[0], raw, local_sem.at[0])
    step_copy = pltpu.make_async_copy(step_hbm, step_ref, local_sem.at[2])
    step_copy.start()
    raw_copy.start()
    has_before = row > 0
    has_after = row < blocks_row - 1

    loop(1, angles, greet)

    cross_after = has_after & (lax.rem(row, 2) == 1)
    cross_before = has_before & (lax.rem(row, 2) == 0)
    chip_after = has_after & (lax.rem(row, 2) == 0)
    chip_before = has_before & (lax.rem(row, 2) == 1)
    first_row = (me == 0) & cross_before
    last_row = (me == angles - 1) & cross_after
    merged = first_row | last_row

    @pl.when(chip_after)
    def _():
        pl.semaphore_signal(barrier, inc=1, device_id={"row": after})

    @pl.when(chip_before)
    def _():
        pl.semaphore_signal(barrier, inc=1, device_id={"row": before})

    @pl.when(first_row)
    def _():
        loop(0, angles, lambda a: pl.semaphore_signal(
            barrier, inc=1, device_id={"angle": a, "row": before}
        ))

    @pl.when(last_row)
    def _():
        loop(0, angles, lambda a: pl.semaphore_signal(
            barrier, inc=1, device_id={"angle": a, "row": after}
        ))

    @pl.when(jnp.logical_not(chip_before))
    def _():
        halo[0] = jnp.zeros_like(halo[0])

    @pl.when(jnp.logical_not(chip_after))
    def _():
        halo[1] = jnp.zeros_like(halo[1])

    table_copy = pltpu.make_async_copy(table_hbm, table, local_sem.at[1])
    table_copy.start()
    partner_copy = pltpu.make_async_copy(partner_hbm, partner_ref, local_sem.at[3])
    partner_copy.start()
    flat_copy = pltpu.make_async_copy(flat_hbm, flat_ref, local_sem.at[4])
    flat_copy.start()
    step_copy.wait()

    def weight(k, values):
        index = step_ref[0, k]
        value = jnp.float32(values[0])
        for i in range(1, steps):
            value = jnp.where(index == i, jnp.float32(values[i]), value)
        return value

    grid = 2.0 * math.pi * np.arange(steps) / steps
    cosines = [weight(k, np.cos(grid).astype(np.float32)) for k in range(steps)]
    sines = [weight(k, np.sin(grid).astype(np.float32)) for k in range(steps)]
    raw_copy.wait()

    def correlate(g):
        at = g * 8 if isinstance(g, int) else pl.multiple_of(g * 8, 8)
        for c in range(chunks):
            sums = [None, None, None]
            for k in range(steps):
                frame = raw[k, pl.ds(at, 8), c * LANES : (c + 1) * LANES].astype(jnp.float32)
                terms = [frame * cosines[k], frame * sines[k], frame]
                sums = terms if k == 0 else [s + t for s, t in zip(sums, terms)]
            for q in range(3):
                corr[q, pl.ds(at * chunks + c, 8, stride=chunks), :] = sums[q]

    loop(0, rows // 8, correlate)

    def halo_copy(side, first, target):
        return pltpu.make_async_remote_copy(
            src_ref=corr.at[:, pl.ds(first * chunks, chunks), :],
            dst_ref=halo.at[side],
            send_sem=halo_send.at[side],
            recv_sem=halo_recv.at[side],
            device_id={"row": target},
        )

    def line(q, i):
        at = i * chunks if isinstance(i, int) else pl.multiple_of(i * chunks, chunks)
        return corr[q, pl.ds(at, chunks), :]

    def ratios(i, lower, upper):
        values = [0.25 * lower(q) + 0.5 * line(q, i) + 0.25 * upper(q) for q in range(3)]
        values = [v.astype(jnp.bfloat16).astype(jnp.float32) for v in values]
        scale = steps / values[2]
        for q in range(2):
            smooth[i, q] = (values[q] * scale).astype(jnp.bfloat16)

    def interior(i):
        ratios(i, lambda q: line(q, i - 1), lambda q: line(q, i + 1))

    loop(1, rows - 1, interior)

    for q in range(3):
        inner = (0.5 * line(q, 0) + 0.25 * line(q, 1), 0.25 * line(q, rows - 2) + 0.5 * line(q, rows - 1))
        outer = (0.25 * line(q, rows - 1), 0.25 * line(q, 0))
        for side in range(2):
            partial[side, q] = inner[side].astype(jnp.bfloat16)
            edge[side, q] = outer[side].astype(jnp.bfloat16)

    pl.semaphore_wait(
        barrier, angles - 1 + has_before.astype(jnp.int32) + has_after.astype(jnp.int32)
    )

    low = halo_copy(0, rows - 1, after)
    high = halo_copy(1, 0, before)

    @pl.when(chip_after)
    def _():
        low.start()

    @pl.when(chip_before)
    def _():
        high.start()

    def row_copy(target):
        return pltpu.make_async_remote_copy(
            src_ref=smooth.at[target],
            dst_ref=recv.at[me],
            send_sem=send_sem.at[target],
            recv_sem=recv_sem.at[me],
            device_id={"angle": target},
        )

    def send(target):
        @pl.when(target != me)
        def _():
            row_copy(target).start()

    def part_copy(side, source):
        return pltpu.make_async_remote_copy(
            src_ref=partial.at[side],
            dst_ref=part.at[source],
            send_sem=send_sem.at[(0, angles - 1)[side]],
            recv_sem=recv_sem.at[source],
            device_id={"angle": (0, angles - 1)[side]},
        )

    def edge_copy(side, source):
        return pltpu.make_async_remote_copy(
            src_ref=edge.at[side],
            dst_ref=extra.at[source],
            send_sem=edge_send.at[side],
            recv_sem=extra_recv.at[source],
            device_id=({"angle": 0, "row": after}, {"angle": angles - 1, "row": before})[side],
        )

    @pl.when(cross_before & (me != 0))
    def _():
        part_copy(0, me).start()

    @pl.when(cross_after)
    def _():
        edge_copy(0, me).start()

    @pl.when(jnp.logical_not(cross_before))
    def _():
        @pl.when(chip_before)
        def _():
            low.wait_recv()

        ratios(0, lambda q: halo[0, q], lambda q: line(q, 1))
        send(0)

    @pl.when(cross_after & (me != angles - 1))
    def _():
        part_copy(1, me).start()

    @pl.when(cross_before)
    def _():
        edge_copy(1, me).start()

    loop(1, angles - 1, send)

    @pl.when(jnp.logical_not(cross_after))
    def _():
        @pl.when(chip_after)
        def _():
            high.wait_recv()

        ratios(rows - 1, lambda q: line(q, rows - 2), lambda q: halo[1, q])
        send(angles - 1)

    @pl.when(jnp.logical_not(merged))
    def _():
        recv[me] = smooth[me]

    @pl.when(first_row)
    def _():
        part[me] = partial[0]

    @pl.when(last_row)
    def _():
        part[me] = partial[1]

    table_copy.wait()
    partner_copy.wait()
    flat_copy.wait()

    def arrived(k):
        source = lax.rem(me + angles - k, angles)
        pltpu.make_async_remote_copy(
            src_ref=smooth.at[source],
            dst_ref=recv.at[source],
            send_sem=send_sem.at[source],
            recv_sem=recv_sem.at[source],
            device_id={"angle": source},
        ).wait_recv()

    def merge(a):
        values = [part[a, q].astype(jnp.float32) + extra[a, q].astype(jnp.float32) for q in range(3)]
        scale = steps / values[2]
        for q in range(2):
            recv[a, q] = (values[q] * scale).astype(jnp.bfloat16)

    @pl.when(jnp.logical_not(merged))
    def _():
        loop(1, angles, arrived)

    for side, here in enumerate((first_row, last_row)):
        @pl.when(here)
        def _():
            loop(1, angles, lambda k: part_copy(side, lax.rem(me + k, angles)).wait_recv())
            loop(0, angles, lambda a: edge_copy(side, a).wait_recv())
            loop(0, angles, merge)


    def spread(a):
        other = partner_ref[a]
        for q in range(2):
            at = a * chunks if isinstance(a, int) else pl.multiple_of(a * chunks, chunks)
            stage[q, pl.ds(at, chunks), :] = recv[a, q].astype(jnp.float32)
            stage[q, pl.ds(at + angles * chunks, chunks), :] = recv[other, q].astype(jnp.float32)

    loop(0, angles, spread)

    flat = flat_ref[...].astype(jnp.float32)
    flat_cos, flat_sin = flat[0:1], flat[1:2]
    for c in range(chunks):
        lanes = slice(c * LANES, (c + 1) * LANES)
        taken = [stage[q, pl.ds(c, 2 * angles, stride=chunks), :] for q in range(2)]
        value = taken[1] * flat_cos[:, lanes] - taken[0] * flat_sin[:, lanes]
        dpc = value.astype(jnp.bfloat16).astype(jnp.float32)
        block = c // (WIDTH // LANES)
        at = (c % (WIDTH // LANES)) * LANES
        ring[(own + block) * angles : (own + block + 1) * angles, at : at + LANES] = dpc[:angles]
        back = own - 1 - block
        mirror[back * angles : (back + 1) * angles, at : at + LANES] = dpc[angles:]

    turns = 2 * own
    flipped = jnp.dot(
        mirror[...].astype(jnp.bfloat16), table[turns], preferred_element_type=jnp.float32
    )
    ring[: own * angles] = flipped
    ring[turns * angles : (turns + own) * angles] = flipped

    total = jnp.zeros((own * angles, WIDTH), jnp.float32)
    for m in range(turns):
        first = (own - m) % turns
        window = ring[first * angles : (first + own) * angles].astype(jnp.bfloat16)
        total = total + jnp.dot(window, table[m], preferred_element_type=jnp.float32)
    for block in range(own):
        out_ref[:, block * WIDTH : (block + 1) * WIDTH] = total[
            block * angles : (block + 1) * angles
        ].astype(jnp.bfloat16)

    def sent(target):
        @pl.when(target != me)
        def _():
            row_copy(target).wait_send()

    loop(1, angles - 1, sent)
    for side, crossing in enumerate((cross_before, cross_after)):
        target = (0, angles - 1)[side]

        @pl.when(jnp.logical_not(crossing))
        def _():
            sent(target)

        @pl.when(crossing & (me != target))
        def _():
            part_copy(side, me).wait_send()

    @pl.when(cross_after)
    def _():
        edge_copy(0, me).wait_send()

    @pl.when(cross_before)
    def _():
        edge_copy(1, me).wait_send()

    @pl.when(chip_after)
    def _():
        low.wait_send()

    @pl.when(chip_before)
    def _():
        high.wait_send()


def local(raw_frames, step_index, partner, flat_field):
    _, steps, rows, det = raw_frames.shape
    angles = lax.axis_size("angle")
    blocks_row = lax.axis_size("row")
    chunks = det // LANES
    own = det // WIDTH
    assert rows == angles and rows % 8 == 0 and raw_frames.shape[0] == 1
    table = jnp.asarray(circulant_blocks(2 * det))
    body = lambda *refs: kernel(angles, blocks_row, *refs)
    result = pl.pallas_call(
        body,
        out_shape=jax.ShapeDtypeStruct((angles, det), jnp.bfloat16),
        in_specs=[pl.BlockSpec(memory_space=pltpu.HBM)] * 5,
        out_specs=pl.BlockSpec(memory_space=pltpu.VMEM),
        scratch_shapes=[
            pltpu.VMEM((steps, rows, det), jnp.bfloat16),
            pltpu.VMEM(table.shape, jnp.bfloat16),
            pltpu.SMEM((1, steps), jnp.int32),
            pltpu.SMEM((angles,), jnp.int32),
            pltpu.VMEM((2, det), jnp.bfloat16),
            pltpu.VMEM((3, rows * chunks, LANES), jnp.float32),
            pltpu.VMEM((2, 3, chunks, LANES), jnp.float32),
            pltpu.VMEM((2, 3, chunks, LANES), jnp.bfloat16),
            pltpu.VMEM((2, 3, chunks, LANES), jnp.bfloat16),
            pltpu.VMEM((angles, 3, chunks, LANES), jnp.bfloat16),
            pltpu.VMEM((angles, 3, chunks, LANES), jnp.bfloat16),
            pltpu.VMEM((rows, 2, chunks, LANES), jnp.bfloat16),
            pltpu.VMEM((angles, 2, chunks, LANES), jnp.bfloat16),
            pltpu.VMEM((2, 2 * angles * chunks, LANES), jnp.float32),
            pltpu.VMEM((own * angles, WIDTH), jnp.float32),
            pltpu.VMEM((3 * own * angles, WIDTH), jnp.float32),
            pltpu.SemaphoreType.DMA((5,)),
            pltpu.SemaphoreType.DMA((2,)),
            pltpu.SemaphoreType.DMA((2,)),
            pltpu.SemaphoreType.DMA((2,)),
            pltpu.SemaphoreType.DMA((angles,)),
            pltpu.SemaphoreType.DMA((angles,)),
            pltpu.SemaphoreType.DMA((angles,)),
        ],
        compiler_params=pltpu.CompilerParams(
            collective_id=0, has_side_effects=True, vmem_limit_bytes=48 * 1024 * 1024
        ),
    )(*[pltpu.with_memory_space_constraint(x, pltpu.HBM) for x in (raw_frames, step_index, partner, flat_field[:, 0, :], table)])
    return result[:, None, :]


def solution(mesh):
    in_specs = (
        P("angle", None, "row", None),
        P("angle", None),
        P(),
        P(None, ("row", "angle"), None),
    )
    out_specs = P(None, ("row", "angle"), None)
    return jax.shard_map(local, mesh=mesh, in_specs=in_specs, out_specs=out_specs, check_vma=False)
```

```python
import math

import jax
import jax.numpy as jnp
import ml_dtypes
import numpy as np
from jax import lax
from jax.experimental import pallas as pl
from jax.experimental.pallas import tpu as pltpu
from jax.sharding import PartitionSpec as P

WIDTH = 256
LANES = 128


def circulant_blocks(padlen):
    count = padlen // WIDTH
    n = np.arange(padlen, dtype=np.float64)
    odd = np.arange(padlen) % 2 == 1
    taps = np.where(odd, (2.0 / padlen) / np.tan(np.pi * np.where(odd, n, 1.0) / padlen), 0.0)
    m = np.arange(count)[:, None, None]
    p = np.arange(WIDTH)[None, :, None]
    q = np.arange(WIDTH)[None, None, :]
    blocks = taps[(WIDTH * m + q - p) % padlen]
    reverse = -np.eye(WIDTH)[::-1][None]
    return np.concatenate([blocks, reverse], axis=0).astype(ml_dtypes.bfloat16)


def loop(start, stop, body):
    if stop - start <= 8:
        for i in range(start, stop):
            body(i)
    else:
        lax.fori_loop(start, stop, lambda i, _: body(i), None)


def kernel(
    angles, blocks_row, raw_hbm, step_hbm, partner_hbm, flat_hbm, table_hbm, out_ref,
    raw, table, step_ref, partner_ref, flat_ref, corr, halo, partial, edge, part, extra, smooth, recv, stage, mirror, ring,
    local_sem, halo_send, halo_recv, edge_send, extra_recv, send_sem, recv_sem,
):
    steps, rows, det = raw.shape
    chunks = det // LANES
    own = det // WIDTH
    me = lax.axis_index("angle")
    row = lax.axis_index("row")
    after = lax.rem(row + 1, blocks_row)
    before = lax.rem(row + blocks_row - 1, blocks_row)

    barrier = pltpu.get_barrier_semaphore()

    def greet(k):
        pl.semaphore_signal(barrier, inc=1, device_id={"angle": lax.rem(me + k, angles)})

    raw_copy = pltpu.make_async_copy(raw_hbm.at[0], raw, local_sem.at[0])
    step_copy = pltpu.make_async_copy(step_hbm, step_ref, local_sem.at[2])
    step_copy.start()
    raw_copy.start()
    has_before = row > 0
    has_after = row < blocks_row - 1

    loop(1, angles, greet)

    cross_after = has_after & (lax.rem(row, 2) == 1)
    cross_before = has_before & (lax.rem(row, 2) == 0)
    chip_after = has_after & (lax.rem(row, 2) == 0)
    chip_before = has_before & (lax.rem(row, 2) == 1)
    first_row = (me == 0) & cross_before
    last_row = (me == angles - 1) & cross_after
    merged = first_row | last_row

    @pl.when(chip_after)
    def _():
        pl.semaphore_signal(barrier, inc=1, device_id={"row": after})

    @pl.when(chip_before)
    def _():
        pl.semaphore_signal(barrier, inc=1, device_id={"row": before})

    @pl.when(first_row)
    def _():
        loop(0, angles, lambda a: pl.semaphore_signal(
            barrier, inc=1, device_id={"angle": a, "row": before}
        ))

    @pl.when(last_row)
    def _():
        loop(0, angles, lambda a: pl.semaphore_signal(
            barrier, inc=1, device_id={"angle": a, "row": after}
        ))

    @pl.when(jnp.logical_not(chip_before))
    def _():
        halo[0] = jnp.zeros_like(halo[0])

    @pl.when(jnp.logical_not(chip_after))
    def _():
        halo[1] = jnp.zeros_like(halo[1])

    table_copy = pltpu.make_async_copy(table_hbm, table, local_sem.at[1])
    table_copy.start()
    partner_copy = pltpu.make_async_copy(partner_hbm, partner_ref, local_sem.at[3])
    partner_copy.start()
    flat_copy = pltpu.make_async_copy(flat_hbm, flat_ref, local_sem.at[4])
    flat_copy.start()
    step_copy.wait()

    def weight(k, values):
        index = step_ref[0, k]
        value = jnp.float32(values[0])
        for i in range(1, steps):
            value = jnp.where(index == i, jnp.float32(values[i]), value)
        return value

    grid = 2.0 * math.pi * np.arange(steps) / steps
    cosines = [weight(k, np.cos(grid).astype(np.float32)) for k in range(steps)]
    sines = [weight(k, np.sin(grid).astype(np.float32)) for k in range(steps)]
    raw_copy.wait()

    def correlate(g):
        at = g * 8 if isinstance(g, int) else pl.multiple_of(g * 8, 8)
        for c in range(chunks):
            sums = [None, None, None]
            for k in range(steps):
                frame = raw[k, pl.ds(at, 8), c * LANES : (c + 1) * LANES].astype(jnp.float32)
                terms = [frame * cosines[k], frame * sines[k], frame]
                sums = terms if k == 0 else [s + t for s, t in zip(sums, terms)]
            for q in range(3):
                corr[q, pl.ds(at * chunks + c, 8, stride=chunks), :] = sums[q]

    loop(0, rows // 8, correlate)

    def halo_copy(side, first, target):
        return pltpu.make_async_remote_copy(
            src_ref=corr.at[:, pl.ds(first * chunks, chunks), :],
            dst_ref=halo.at[side],
            send_sem=halo_send.at[side],
            recv_sem=halo_recv.at[side],
            device_id={"row": target},
        )

    def line(q, i):
        at = i * chunks if isinstance(i, int) else pl.multiple_of(i * chunks, chunks)
        return corr[q, pl.ds(at, chunks), :]

    def ratios(i, lower, upper):
        values = [0.25 * lower(q) + 0.5 * line(q, i) + 0.25 * upper(q) for q in range(3)]
        values = [v.astype(jnp.bfloat16).astype(jnp.float32) for v in values]
        scale = steps / values[2]
        for q in range(2):
            smooth[i, q] = (values[q] * scale).astype(jnp.bfloat16)

    def interior(i):
        ratios(i, lambda q: line(q, i - 1), lambda q: line(q, i + 1))

    loop(1, rows - 1, interior)

    @pl.when(jnp.logical_not(has_before))
    def _():
        ratios(0, lambda q: halo[0, q], lambda q: line(q, 1))

    @pl.when(jnp.logical_not(has_after))
    def _():
        ratios(rows - 1, lambda q: line(q, rows - 2), lambda q: halo[1, q])

    for q in range(3):
        inner = (0.5 * line(q, 0) + 0.25 * line(q, 1), 0.25 * line(q, rows - 2) + 0.5 * line(q, rows - 1))
        outer = (0.25 * line(q, rows - 1), 0.25 * line(q, 0))
        for side in range(2):
            partial[side, q] = inner[side].astype(jnp.bfloat16)
            edge[side, q] = outer[side].astype(jnp.bfloat16)

    pl.semaphore_wait(
        barrier, angles - 1 + has_before.astype(jnp.int32) + has_after.astype(jnp.int32)
    )

    low = halo_copy(0, rows - 1, after)
    high = halo_copy(1, 0, before)

    @pl.when(chip_after)
    def _():
        low.start()

    @pl.when(chip_before)
    def _():
        high.start()

    def row_copy(target):
        return pltpu.make_async_remote_copy(
            src_ref=smooth.at[target],
            dst_ref=recv.at[me],
            send_sem=send_sem.at[target],
            recv_sem=recv_sem.at[me],
            device_id={"angle": target},
        )

    def send(target):
        @pl.when(target != me)
        def _():
            row_copy(target).start()

    def part_copy(side, source):
        return pltpu.make_async_remote_copy(
            src_ref=partial.at[side],
            dst_ref=part.at[source],
            send_sem=send_sem.at[(0, angles - 1)[side]],
            recv_sem=recv_sem.at[source],
            device_id={"angle": (0, angles - 1)[side]},
        )

    def edge_copy(side, source):
        return pltpu.make_async_remote_copy(
            src_ref=edge.at[side],
            dst_ref=extra.at[source],
            send_sem=edge_send.at[side],
            recv_sem=extra_recv.at[source],
            device_id=({"angle": 0, "row": after}, {"angle": angles - 1, "row": before})[side],
        )

    @pl.when(cross_before & (me != 0))
    def _():
        part_copy(0, me).start()

    @pl.when(cross_after)
    def _():
        edge_copy(0, me).start()

    @pl.when(jnp.logical_not(cross_before))
    def _():
        @pl.when(chip_before)
        def _():
            low.wait_recv()
            ratios(0, lambda q: halo[0, q], lambda q: line(q, 1))

        send(0)

    @pl.when(cross_after & (me != angles - 1))
    def _():
        part_copy(1, me).start()

    @pl.when(cross_before)
    def _():
        edge_copy(1, me).start()

    loop(1, angles - 1, send)

    @pl.when(jnp.logical_not(cross_after))
    def _():
        @pl.when(chip_after)
        def _():
            high.wait_recv()
            ratios(rows - 1, lambda q: line(q, rows - 2), lambda q: halo[1, q])

        send(angles - 1)

    @pl.when(jnp.logical_not(merged))
    def _():
        recv[me] = smooth[me]

    @pl.when(first_row)
    def _():
        part[me] = partial[0]

    @pl.when(last_row)
    def _():
        part[me] = partial[1]

    table_copy.wait()
    partner_copy.wait()
    flat_copy.wait()

    def arrived(k):
        source = lax.rem(me + angles - k, angles)
        pltpu.make_async_remote_copy(
            src_ref=smooth.at[source],
            dst_ref=recv.at[source],
            send_sem=send_sem.at[source],
            recv_sem=recv_sem.at[source],
            device_id={"angle": source},
        ).wait_recv()

    def merge(a):
        values = [part[a, q].astype(jnp.float32) + extra[a, q].astype(jnp.float32) for q in range(3)]
        scale = steps / values[2]
        for q in range(2):
            recv[a, q] = (values[q] * scale).astype(jnp.bfloat16)

    @pl.when(jnp.logical_not(merged))
    def _():
        loop(1, angles, arrived)

    for side, here in enumerate((first_row, last_row)):
        @pl.when(here)
        def _():
            loop(1, angles, lambda k: part_copy(side, lax.rem(me + k, angles)).wait_recv())
            loop(0, angles, lambda a: edge_copy(side, a).wait_recv())
            loop(0, angles, merge)


    def spread(a):
        other = partner_ref[a]
        for q in range(2):
            at = a * chunks if isinstance(a, int) else pl.multiple_of(a * chunks, chunks)
            stage[q, pl.ds(at, chunks), :] = recv[a, q].astype(jnp.float32)
            stage[q, pl.ds(at + angles * chunks, chunks), :] = recv[other, q].astype(jnp.float32)

    loop(0, angles, spread)

    flat = flat_ref[...].astype(jnp.float32)
    flat_cos, flat_sin = flat[0:1], flat[1:2]
    for c in range(chunks):
        lanes = slice(c * LANES, (c + 1) * LANES)
        taken = [stage[q, pl.ds(c, 2 * angles, stride=chunks), :] for q in range(2)]
        value = taken[1] * flat_cos[:, lanes] - taken[0] * flat_sin[:, lanes]
        dpc = value.astype(jnp.bfloat16).astype(jnp.float32)
        block = c // (WIDTH // LANES)
        at = (c % (WIDTH // LANES)) * LANES
        ring[(own + block) * angles : (own + block + 1) * angles, at : at + LANES] = dpc[:angles]
        back = own - 1 - block
        mirror[back * angles : (back + 1) * angles, at : at + LANES] = dpc[angles:]

    turns = 2 * own
    flipped = jnp.dot(
        mirror[...].astype(jnp.bfloat16), table[turns], preferred_element_type=jnp.float32
    )
    ring[: own * angles] = flipped
    ring[turns * angles : (turns + own) * angles] = flipped

    total = jnp.zeros((own * angles, WIDTH), jnp.float32)
    for m in range(turns):
        first = (own - m) % turns
        window = ring[first * angles : (first + own) * angles].astype(jnp.bfloat16)
        total = total + jnp.dot(window, table[m], preferred_element_type=jnp.float32)
    for block in range(own):
        out_ref[:, block * WIDTH : (block + 1) * WIDTH] = total[
            block * angles : (block + 1) * angles
        ].astype(jnp.bfloat16)

    def sent(target):
        @pl.when(target != me)
        def _():
            row_copy(target).wait_send()

    loop(1, angles - 1, sent)
    for side, crossing in enumerate((cross_before, cross_after)):
        target = (0, angles - 1)[side]

        @pl.when(jnp.logical_not(crossing))
        def _():
            sent(target)

        @pl.when(crossing & (me != target))
        def _():
            part_copy(side, me).wait_send()

    @pl.when(cross_after)
    def _():
        edge_copy(0, me).wait_send()

    @pl.when(cross_before)
    def _():
        edge_copy(1, me).wait_send()

    @pl.when(chip_after)
    def _():
        low.wait_send()

    @pl.when(chip_before)
    def _():
        high.wait_send()


def local(raw_frames, step_index, partner, flat_field):
    _, steps, rows, det = raw_frames.shape
    angles = lax.axis_size("angle")
    blocks_row = lax.axis_size("row")
    chunks = det // LANES
    own = det // WIDTH
    assert rows == angles and rows % 8 == 0 and raw_frames.shape[0] == 1
    table = jnp.asarray(circulant_blocks(2 * det))
    body = lambda *refs: kernel(angles, blocks_row, *refs)
    result = pl.pallas_call(
        body,
        out_shape=jax.ShapeDtypeStruct((angles, det), jnp.bfloat16),
        in_specs=[pl.BlockSpec(memory_space=pltpu.HBM)] * 5,
        out_specs=pl.BlockSpec(memory_space=pltpu.VMEM),
        scratch_shapes=[
            pltpu.VMEM((steps, rows, det), jnp.bfloat16),
            pltpu.VMEM(table.shape, jnp.bfloat16),
            pltpu.SMEM((1, steps), jnp.int32),
            pltpu.SMEM((angles,), jnp.int32),
            pltpu.VMEM((2, det), jnp.bfloat16),
            pltpu.VMEM((3, rows * chunks, LANES), jnp.float32),
            pltpu.VMEM((2, 3, chunks, LANES), jnp.float32),
            pltpu.VMEM((2, 3, chunks, LANES), jnp.bfloat16),
            pltpu.VMEM((2, 3, chunks, LANES), jnp.bfloat16),
            pltpu.VMEM((angles, 3, chunks, LANES), jnp.bfloat16),
            pltpu.VMEM((angles, 3, chunks, LANES), jnp.bfloat16),
            pltpu.VMEM((rows, 2, chunks, LANES), jnp.bfloat16),
            pltpu.VMEM((angles, 2, chunks, LANES), jnp.bfloat16),
            pltpu.VMEM((2, 2 * angles * chunks, LANES), jnp.float32),
            pltpu.VMEM((own * angles, WIDTH), jnp.float32),
            pltpu.VMEM((3 * own * angles, WIDTH), jnp.float32),
            pltpu.SemaphoreType.DMA((5,)),
            pltpu.SemaphoreType.DMA((2,)),
            pltpu.SemaphoreType.DMA((2,)),
            pltpu.SemaphoreType.DMA((2,)),
            pltpu.SemaphoreType.DMA((angles,)),
            pltpu.SemaphoreType.DMA((angles,)),
            pltpu.SemaphoreType.DMA((angles,)),
        ],
        compiler_params=pltpu.CompilerParams(
            collective_id=0, has_side_effects=True, vmem_limit_bytes=48 * 1024 * 1024
        ),
    )(*[pltpu.with_memory_space_constraint(x, pltpu.HBM) for x in (raw_frames, step_index, partner, flat_field[:, 0, :], table)])
    return result[:, None, :]


def solution(mesh):
    in_specs = (
        P("angle", None, "row", None),
        P("angle", None),
        P(),
        P(None, ("row", "angle"), None),
    )
    out_specs = P(None, ("row", "angle"), None)
    return jax.shard_map(local, mesh=mesh, in_specs=in_specs, out_specs=out_specs, check_vma=False)
```
